32 devices in a mesh: dp: 16 (over z, y, core), tensor: 2 (over x).
Axes of the slice: x: 2, y: 2, z: 4, core: 2. Of those that a mesh axis runs over, the one named last changes fastest.
Arguments:
- tokens: bfloat16 [8192, 640], P(('dp', 'tensor')), may hold values from -40 to 40
- segment_ids: int32 [8192], P('dp'), may hold values from 0 to 8, as said below
- query_weight: bfloat16 [640, 1024], P('dp', 'tensor'), may hold values from -1 to 1
- key_weight: bfloat16 [640, 256], P('dp'), may hold values from -1 to 1
- value_weight: bfloat16 [640, 256], P('dp'), may hold values from -0.25 to 0.25
- out_weight: bfloat16 [1024, 640], P('tensor', 'dp'), may hold values from -1 to 1
- gate_weight: bfloat16 [640, 2048], P('dp', 'tensor'), may hold values from -0.25 to 0.25
- up_weight: bfloat16 [640, 2048], P('dp', 'tensor'), may hold values from -0.25 to 0.25
- down_weight: bfloat16 [2048, 640], P('tensor', 'dp'), may hold values from -1 to 1
- gain_before_attention: bfloat16 [640], P('dp'), may hold values from 0.25 to 1.75
- gain_after_attention: bfloat16 [640], P('dp'), may hold values from 0.25 to 1.75
- gain_before_feed: bfloat16 [640], P('dp'), may hold values from 0.25 to 1.75
- gain_after_feed: bfloat16 [640], P('dp'), may hold values from 0.25 to 1.75
- query_gain: bfloat16 [256], P('dp'), may hold values from 0.25 to 1.75
- key_gain: bfloat16 [256], P('dp'), may hold values from 0.25 to 1.75
- cotangent: float32 [8192, 640], P(('dp', 'tensor')), may hold values from -6 to 6
Outputs:
- outputs: float32 [8192, 640], P(('dp', 'tensor'))
- tokens_grad: float32 [8192, 640], P(('dp', 'tensor'))
- query_weight_grad: float32 [640, 1024], P('dp', 'tensor')
- key_weight_grad: float32 [640, 256], P('dp')
- value_weight_grad: float32 [640, 256], P('dp')
- out_weight_grad: float32 [1024, 640], P('tensor', 'dp')
- gate_weight_grad: float32 [640, 2048], P('dp', 'tensor')
- up_weight_grad: float32 [640, 2048], P('dp', 'tensor')
- down_weight_grad: float32 [2048, 640], P('tensor', 'dp')
- gain_before_attention_grad: float32 [640], P('dp')
- gain_after_attention_grad: float32 [640], P('dp')
- gain_before_feed_grad: float32 [640], P('dp')
- gain_after_feed_grad: float32 [640], P('dp')
- query_gain_grad: float32 [256], P('dp')
- key_gain_grad: float32 [256], P('dp')
The draws below stay inside these ranges and needn't reach their ends.
Inputs may be any that keep to these rules, and one draw needn't show every extreme that they name: `segment_ids`: within each aligned block of 512 tokens the numbers never fall; a document is a run of equal numbers inside one such block; in some block one document fills all 512 tokens.
All inputs are finite; a program needn't handle non-finite values.
Results may differ from the reference program's by a relative error of at most 0.019.
Values may be sent and summed in bfloat16 or wider, within the bound.
A program may use at most 128 MiB of HBM per device.

```python
import math
import jax
import jax.numpy as jnp
from jax import lax

D = 640
H = 4
HD = 256
FF = 2048
WINDOW = 512
TOK_DEV = 512
TOKENS = 8192


def column_scaled(key, row_total, col_total, fan):
    key_base, key_scale = jax.random.split(key)
    base = jnp.clip(jax.random.normal(key_base, (row_total, col_total), jnp.float32), -4.0, 4.0)
    scales = jnp.exp(jax.random.uniform(key_scale, (col_total,), jnp.float32, math.log(0.3), math.log(3.0)))
    return (base * scales[None, :] / math.sqrt(fan)).astype(jnp.bfloat16)


def draw_query_weight(key, part):
    return column_scaled(jax.random.fold_in(key, 11), D, H * HD, D)


def draw_key_weight(key, part):
    return column_scaled(jax.random.fold_in(key, 12), D, HD, D)


def draw_out_weight(key, part):
    return column_scaled(jax.random.fold_in(key, 13), H * HD, D, H * HD)


def draw_down_weight(key, part):
    return column_scaled(jax.random.fold_in(key, 14), FF, D, FF)


def draw_tokens(key, part):
    key_base, key_row, key_col = jax.random.split(jax.random.fold_in(key, 21), 3)
    row_scale = jnp.exp(jax.random.uniform(key_row, (TOKENS, 1), jnp.float32, math.log(0.3), math.log(3.0)))
    col_scale = jnp.exp(jax.random.uniform(key_col, (1, D), jnp.float32, math.log(0.3), math.log(3.0)))
    base = jnp.clip(jax.random.normal(key_base, (TOKENS, D), jnp.float32), -4.0, 4.0)
    return (base * row_scale * col_scale).astype(jnp.bfloat16)


def draw_segment_ids(key, part):
    block_total = TOKENS // TOK_DEV
    key_count, key_cut, key_full = jax.random.split(jax.random.fold_in(key, 31), 3)
    cut_number = jax.random.randint(key_count, (block_total,), 0, 9)
    whole_block = jax.random.randint(key_full, (), 0, block_total)
    block_ids = jnp.arange(block_total, dtype=jnp.int32)
    cut_number = jnp.where(block_ids == (whole_block + 1) % block_total, 8, cut_number)
    cut_place = jax.random.randint(key_cut, (block_total, 8), 1, TOK_DEV)
    slot_ids = jnp.arange(8, dtype=jnp.int32)
    valid = (slot_ids[None, :] < cut_number[:, None]) & (block_ids[:, None] != whole_block)
    positions = jnp.arange(TOK_DEV, dtype=jnp.int32)
    passed = valid[:, :, None] & (cut_place[:, :, None] <= positions[None, None, :])
    local_ids = jnp.sum(passed.astype(jnp.int32), axis=1)
    return local_ids.reshape(TOKENS).astype(jnp.int32)


def spiked(values, rng, source, target, shards_of, factor):
    owner, partner = [(jnp.arange(values.shape[position]) // (values.shape[position] // shards_of)).reshape([-1 if axis == position else 1 for axis in range(values.ndim)]) for position in (source, target)]
    chosen = jax.random.permutation(rng, shards_of)[partner]
    strong = (owner == chosen) | (owner == (partner + shards_of // 2) % shards_of)
    return jnp.where(strong, factor * values, values)


def block_scale(key, dims, pieces, least, high):
    level, own = 1.0, jax.random.fold_in(key, 6)
    for dim, blocks in pieces:
        heights = jnp.exp(jax.random.uniform(jax.random.fold_in(own, dim), (blocks,), jnp.float32, least / len(pieces), high / len(pieces)))
        level = level * jnp.repeat(heights, dims[dim] // blocks).reshape([-1 if axis == dim else 1 for axis in range(len(dims))])
    return level


def centred(rng, extent, width, most, pieces=(), kind=jnp.bfloat16):
    level = block_scale(rng, extent, pieces, -0.22, 0.18) if pieces else 1.0
    drawn = jax.random.normal(rng, extent, jnp.float32) * width * level
    return jnp.minimum(jnp.maximum(drawn, -most), most).astype(kind)


def bell_draw_with(rng, shape, deviation, limit, cuts, heavy, held_as=jnp.bfloat16):
    array = deviation * jax.random.normal(rng, shape, jnp.float32)
    if cuts:
        array = array * block_scale(rng, shape, cuts, -0.22, 0.18)
    return jnp.clip(spiked(array, jax.random.fold_in(rng, 3), *heavy), -limit, limit).astype(held_as)


def setup_inputs(seed: int = 0) -> dict:
    key_of = jax.random.split(jax.random.key(seed), 17)
    tokens = draw_tokens(jax.random.fold_in(key_of[16], 71), 0)
    segment_ids = draw_segment_ids(jax.random.fold_in(key_of[16], 71), 0)
    query_weight = draw_query_weight(jax.random.fold_in(key_of[16], 71), 0)
    key_weight = draw_key_weight(jax.random.fold_in(key_of[16], 71), 0)
    value_weight = centred(key_of[4], (D, HD), D ** -0.5, 0.25, ((0, 16),))
    out_weight = draw_out_weight(jax.random.fold_in(key_of[16], 71), 0)
    gate_weight = centred(key_of[6], (D, FF), D ** -0.5, 0.25, ((0, 16), (1, 2)))
    up_weight = centred(key_of[7], (D, FF), D ** -0.5, 0.25, ((0, 16), (1, 2)))
    down_weight = draw_down_weight(jax.random.fold_in(key_of[16], 71), 0)
    gain_before_attention = jnp.clip(1.0 + 0.15 * jax.random.normal(key_of[9], (D,), jnp.float32), 0.25, 1.75).astype(jnp.bfloat16)
    gain_after_attention = jnp.clip(1.0 + 0.15 * jax.random.normal(key_of[10], (D,), jnp.float32), 0.25, 1.75).astype(jnp.bfloat16)
    gain_before_feed = jnp.clip(1.0 + 0.15 * jax.random.normal(key_of[11], (D,), jnp.float32), 0.25, 1.75).astype(jnp.bfloat16)
    gain_after_feed = jnp.clip(1.0 + 0.15 * jax.random.normal(key_of[12], (D,), jnp.float32), 0.25, 1.75).astype(jnp.bfloat16)
    query_gain = jnp.clip(1.0 + 0.15 * jax.random.normal(key_of[13], (HD,), jnp.float32), 0.25, 1.75).astype(jnp.bfloat16)
    key_gain = jnp.clip(1.0 + 0.15 * jax.random.normal(key_of[14], (HD,), jnp.float32), 0.25, 1.75).astype(jnp.bfloat16)
    cotangent = bell_draw_with(key_of[15], (TOKENS, D), 1.0, 6.0, ((0, 32),), (0, 1, 32, 2.75), jnp.float32)
    return dict(tokens=tokens, segment_ids=segment_ids, query_weight=query_weight, key_weight=key_weight, value_weight=value_weight, out_weight=out_weight, gate_weight=gate_weight, up_weight=up_weight, down_weight=down_weight, gain_before_attention=gain_before_attention, gain_after_attention=gain_after_attention, gain_before_feed=gain_before_feed, gain_after_feed=gain_after_feed, query_gain=query_gain, key_gain=key_gain, cotangent=cotangent)


EPS = 1e-06
ROPE_BASE = 10000.0

def norm_fwd(values, gain):
    inverse = lax.rsqrt(lax.optimization_barrier(jnp.mean(values * values, axis=-1, keepdims=True)) + EPS)
    return values * inverse * gain

def norm_back(values, gain, grad_out):
    inverse = lax.rsqrt(lax.optimization_barrier(jnp.mean(values * values, axis=-1, keepdims=True)) + EPS)
    unit_rows = values * inverse
    scaled = grad_out * gain
    grad_in = inverse * (scaled - unit_rows * lax.optimization_barrier(jnp.mean(scaled * unit_rows, axis=-1, keepdims=True)))
    grad_gain = lax.optimization_barrier(jnp.sum((grad_out * unit_rows).reshape(-1, values.shape[-1]), axis=0))
    return (grad_in, grad_gain)

def gelu_parts(gate_pre):
    factor = math.sqrt(2.0 / math.pi)
    tangent = jnp.tanh(factor * (gate_pre + 0.044715 * gate_pre * gate_pre * gate_pre))
    value_out = 0.5 * gate_pre * (1.0 + tangent)
    slope = 0.5 * (1.0 + tangent) + 0.5 * gate_pre * (1.0 - tangent * tangent) * factor * (1.0 + 3.0 * 0.044715 * gate_pre * gate_pre)
    return (value_out, slope)

def rope_tables(segments):
    earlier = lax.optimization_barrier(jnp.sum((segments[None, :] < segments[:, None]).astype(jnp.int32), axis=1))
    place = (jnp.arange(segments.shape[0], dtype=jnp.int32) - earlier).astype(jnp.float32)
    half_width = HD // 2
    freq = jnp.exp(-(2.0 * jnp.arange(half_width, dtype=jnp.float32) / HD) * math.log(ROPE_BASE))
    angle = place[:, None] * freq[None, :]
    return (jnp.cos(angle), jnp.sin(angle))

def rotate(vals, cosine, sine_table):
    half_width = vals.shape[-1] // 2
    first_half = vals[..., :half_width]
    second = vals[..., half_width:]
    return jnp.concatenate([first_half * cosine - second * sine_table, second * cosine + first_half * sine_table], axis=-1)

def unrotate(grads, cosine, sine_table):
    half_width = grads.shape[-1] // 2
    first_half = grads[..., :half_width]
    second = grads[..., half_width:]
    return jnp.concatenate([first_half * cosine + second * sine_table, second * cosine - first_half * sine_table], axis=-1)

def allowed_pairs(seg_query, seg_key, query_first, key_first):
    query_pos = query_first + jnp.arange(seg_query.shape[0], dtype=jnp.int32)
    key_pos = key_first + jnp.arange(seg_key.shape[0], dtype=jnp.int32)
    spacing = query_pos[:, None] - key_pos[None, :]
    return (seg_query[:, None] == seg_key[None, :]) & (spacing >= 0) & (spacing < WINDOW)

def reference(tokens, segment_ids, query_weight, key_weight, value_weight, out_weight, gate_weight, up_weight, down_weight, gain_before_attention, gain_after_attention, gain_before_feed, gain_after_feed, query_gain, key_gain, cotangent):
    f32 = jnp.float32
    bf16 = jnp.bfloat16
    blocks = TOKENS // TOK_DEV
    scale = HD ** (-0.5)
    gain_ai = gain_before_attention.astype(f32)
    gain_ao = gain_after_attention.astype(f32)
    gain_fi = gain_before_feed.astype(f32)
    gain_fo = gain_after_feed.astype(f32)
    gain_query = query_gain.astype(f32)
    gain_key = key_gain.astype(f32)
    zeros = (jnp.zeros((D, H * HD), f32), jnp.zeros((D, HD), f32), jnp.zeros((D, HD), f32), jnp.zeros((H * HD, D), f32), jnp.zeros((D, FF), f32), jnp.zeros((D, FF), f32), jnp.zeros((FF, D), f32), jnp.zeros((D,), f32), jnp.zeros((D,), f32), jnp.zeros((D,), f32), jnp.zeros((D,), f32), jnp.zeros((HD,), f32), jnp.zeros((HD,), f32))

    def one_block(totals, inputs):
        tok_block, seg_block, cot_block = inputs
        x_rows = tok_block.astype(f32)
        normed_in = norm_fwd(x_rows, gain_ai).astype(bf16)
        queries = jnp.dot(normed_in, query_weight, preferred_element_type=f32).reshape(TOK_DEV, H, HD)
        key_rows = jnp.dot(normed_in, key_weight, preferred_element_type=f32)
        value_rows = jnp.dot(normed_in, value_weight, preferred_element_type=f32).astype(bf16)
        cosine, sine_table = rope_tables(seg_block)
        query_rot = (rotate(norm_fwd(queries, gain_query), cosine[:, None, :], sine_table[:, None, :]) * scale).astype(bf16)
        key_rot = rotate(norm_fwd(key_rows, gain_key), cosine, sine_table).astype(bf16)
        allowed = allowed_pairs(seg_block, seg_block, 0, 0)[None]
        scores = jnp.einsum('qhd,kd->hqk', query_rot.astype(f32), key_rot.astype(f32))
        exp_total = lax.optimization_barrier(jnp.sum(jnp.where(allowed, jnp.exp(scores), 0.0), axis=-1, keepdims=True))
        log_total = jnp.log(exp_total)
        probs = jnp.where(allowed, jnp.exp(scores - log_total), 0.0)
        probs_b = probs.astype(bf16)
        attended = jnp.einsum('hqk,kd->qhd', probs_b.astype(f32), value_rows.astype(f32)).reshape(TOK_DEV, H * HD).astype(bf16)
        mixed = jnp.dot(attended, out_weight, preferred_element_type=f32)
        hidden_state = x_rows + norm_fwd(mixed, gain_ao)
        normed_mid = norm_fwd(hidden_state, gain_fi).astype(bf16)
        gate_pre = jnp.dot(normed_mid, gate_weight, preferred_element_type=f32)
        up_values = jnp.dot(normed_mid, up_weight, preferred_element_type=f32)
        gelu_value, gelu_slope = gelu_parts(gate_pre)
        activated = (gelu_value * up_values).astype(bf16)
        feed_out = jnp.dot(activated, down_weight, preferred_element_type=f32)
        result = hidden_state + norm_fwd(feed_out, gain_fo)
        grad_feed, grad_gfo = norm_back(feed_out, gain_fo, cot_block)
        grad_feed_b = grad_feed.astype(bf16)
        grad_act = jnp.dot(grad_feed_b, down_weight.T, preferred_element_type=f32)
        grad_down = jnp.dot(activated.T, grad_feed_b, preferred_element_type=f32)
        grad_gate_b = (grad_act * up_values * gelu_slope).astype(bf16)
        grad_up_b = (grad_act * gelu_value).astype(bf16)
        grad_gate_w = jnp.dot(normed_mid.T, grad_gate_b, preferred_element_type=f32)
        grad_up_w = jnp.dot(normed_mid.T, grad_up_b, preferred_element_type=f32)
        grad_mid = jnp.dot(grad_gate_b, gate_weight.T, preferred_element_type=f32) + jnp.dot(grad_up_b, up_weight.T, preferred_element_type=f32)
        grad_mid_in, grad_gfi = norm_back(hidden_state, gain_fi, grad_mid)
        grad_hidden = cot_block + grad_mid_in
        grad_mixed, grad_gao = norm_back(mixed, gain_ao, grad_hidden)
        grad_mixed_b = grad_mixed.astype(bf16)
        grad_attended = jnp.dot(grad_mixed_b, out_weight.T, preferred_element_type=f32).astype(bf16)
        grad_out_w = jnp.dot(attended.T, grad_mixed_b, preferred_element_type=f32)
        grad_heads = grad_attended.reshape(TOK_DEV, H, HD).astype(f32)
        grad_probs = jnp.einsum('qhd,kd->hqk', grad_heads, value_rows.astype(f32))
        grad_scores = (probs * (grad_probs - lax.optimization_barrier(jnp.sum(probs * grad_probs, axis=-1, keepdims=True)))).astype(bf16).astype(f32)
        grad_qrot = jnp.einsum('hqk,kd->qhd', grad_scores, key_rot.astype(f32))
        grad_krot = jnp.einsum('hqk,qhd->kd', grad_scores, query_rot.astype(f32))
        grad_value_b = jnp.einsum('hqk,qhd->kd', probs_b.astype(f32), grad_heads).astype(bf16)
        grad_qunit = unrotate(grad_qrot * scale, cosine[:, None, :], sine_table[:, None, :])
        grad_kunit = unrotate(grad_krot, cosine, sine_table)
        grad_queries, grad_gq = norm_back(queries, gain_query, grad_qunit)
        grad_keys, grad_gk = norm_back(key_rows, gain_key, grad_kunit)
        grad_queries_b = grad_queries.reshape(TOK_DEV, H * HD).astype(bf16)
        grad_keys_b = grad_keys.astype(bf16)
        grad_query_w = jnp.dot(normed_in.T, grad_queries_b, preferred_element_type=f32)
        grad_key_w = jnp.dot(normed_in.T, grad_keys_b, preferred_element_type=f32)
        grad_value_w = jnp.dot(normed_in.T, grad_value_b, preferred_element_type=f32)
        grad_normed = jnp.dot(grad_queries_b, query_weight.T, preferred_element_type=f32) + jnp.dot(grad_keys_b, key_weight.T, preferred_element_type=f32) + jnp.dot(grad_value_b, value_weight.T, preferred_element_type=f32)
        grad_in_rows, grad_gai = norm_back(x_rows, gain_ai, grad_normed)
        grad_tokens = grad_hidden + grad_in_rows
        terms = (grad_query_w, grad_key_w, grad_value_w, grad_out_w, grad_gate_w, grad_up_w, grad_down, grad_gai, grad_gao, grad_gfi, grad_gfo, grad_gq, grad_gk)
        new_totals = tuple((total + term for total, term in zip(totals, terms)))
        return (new_totals, (result, grad_tokens))
    totals, (results, grads_in) = lax.scan(one_block, zeros, (tokens.reshape(blocks, TOK_DEV, D), segment_ids.reshape(blocks, TOK_DEV), cotangent.reshape(blocks, TOK_DEV, D)))
    return (results.reshape(TOKENS, D), grads_in.reshape(TOKENS, D), totals[0], totals[1], totals[2], totals[3], totals[4], totals[5], totals[6], totals[7], totals[8], totals[9], totals[10], totals[11], totals[12])
```

```python
import math

import jax
import jax.numpy as jnp
from jax import lax
from jax.experimental import pallas as pl
from jax.experimental.pallas import tpu as pltpu
from jax.sharding import PartitionSpec as P

HD = 256
WINDOW = 512


EPS = 1e-06
ROPE_BASE = 10000.0


def norm_fwd(values, gain):
    inverse = lax.rsqrt(jnp.mean(values * values, axis=-1, keepdims=True) + EPS)
    return values * inverse * gain


def norm_back(values, gain, grad_out):
    inverse = lax.rsqrt(jnp.mean(values * values, axis=-1, keepdims=True) + EPS)
    unit_rows = values * inverse
    scaled = grad_out * gain
    grad_in = inverse * (scaled - unit_rows * jnp.mean(scaled * unit_rows, axis=-1, keepdims=True))
    grad_gain = jnp.sum((grad_out * unit_rows).reshape(-1, values.shape[-1]), axis=0)
    return (grad_in, grad_gain)


def gelu_parts(gate_pre):
    factor = math.sqrt(2.0 / math.pi)
    tangent = jnp.tanh(factor * (gate_pre + 0.044715 * gate_pre * gate_pre * gate_pre))
    value_out = 0.5 * gate_pre * (1.0 + tangent)
    slope = 0.5 * (1.0 + tangent) + 0.5 * gate_pre * (1.0 - tangent * tangent) * factor * (
        1.0 + 3.0 * 0.044715 * gate_pre * gate_pre
    )
    return (value_out, slope)


def rope_tables(segments, position):
    earlier = jnp.sum((segments[None, :] < segments[:, None]).astype(jnp.int32), axis=1)
    place = (position - earlier).astype(jnp.float32)
    half_width = HD // 2
    freq = jnp.exp(-(2.0 * jnp.arange(half_width, dtype=jnp.float32) / HD) * math.log(ROPE_BASE))
    angle = place[:, None] * freq[None, :]
    return (jnp.cos(angle), jnp.sin(angle))


def rotate(vals, cosine, sine_table):
    half_width = vals.shape[-1] // 2
    first_half = vals[..., :half_width]
    second = vals[..., half_width:]
    return jnp.concatenate(
        [first_half * cosine - second * sine_table, second * cosine + first_half * sine_table],
        axis=-1,
    )


def unrotate(grads, cosine, sine_table):
    half_width = grads.shape[-1] // 2
    first_half = grads[..., :half_width]
    second = grads[..., half_width:]
    return jnp.concatenate(
        [first_half * cosine + second * sine_table, second * cosine - first_half * sine_table],
        axis=-1,
    )


def greet(partners):
    barrier = pltpu.get_barrier_semaphore()
    for axis, index in partners:
        pl.semaphore_signal(
            barrier, inc=1, device_id={axis: index}, device_id_type=pl.DeviceIdType.MESH
        )
    pl.semaphore_wait(barrier, len(partners))


def dp_place(size):
    me = lax.axis_index("dp")
    core = lax.rem(me, 2)
    side = lax.rem(me // 2, 2)
    depth = me // 4
    return me, depth, side, core


def dp_index(depth, side, core):
    return depth * 4 + side * 2 + core


def remote(src, dst, send, recv, index):
    return pltpu.make_async_remote_copy(
        src_ref=src,
        dst_ref=dst,
        send_sem=send,
        recv_sem=recv,
        device_id={"dp": index},
        device_id_type=pl.DeviceIdType.MESH,
    )


def gather_kernel(layers, own_ref, full_ref, z_send, z_recv, y_send, y_recv, c_send, c_recv, local):
    me, depth, side, core = dp_place(layers * 4)
    deeper = [lax.rem(depth + step, layers) for step in range(1, layers)]
    y_peer = dp_index(depth, 1 - side, core)
    c_peer = dp_index(depth, side, 1 - core)
    greet([("dp", dp_index(d, side, core)) for d in deeper] + [("dp", y_peer), ("dp", c_peer)])
    sends = []

    def start(src, index, send, recv, target):
        copy = remote(src, full_ref.at[index], send, recv, target)
        copy.start()
        sends.append(copy)

    def arrived(index, recv):
        remote(full_ref.at[index], full_ref.at[index], local, recv, y_peer).wait_recv()

    keep = pltpu.make_async_copy(own_ref, full_ref.at[me], local)
    keep.start()
    start(own_ref, me, y_send.at[depth], y_recv.at[depth], y_peer)
    for d in deeper:
        start(own_ref, me, z_send.at[d], z_recv.at[depth], dp_index(d, side, core))
    start(own_ref, me, c_send.at[2 * depth + side], c_recv.at[2 * depth + side], c_peer)
    for d in deeper:
        index = dp_index(d, side, core)
        arrived(index, z_recv.at[d])
        start(full_ref.at[index], index, y_send.at[d], y_recv.at[d], y_peer)
        slot = 2 * d + side
        start(full_ref.at[index], index, c_send.at[slot], c_recv.at[slot], c_peer)
    for d in [depth] + deeper:
        index = dp_index(d, 1 - side, core)
        arrived(index, y_recv.at[d])
        slot = 2 * d + 1 - side
        start(full_ref.at[index], index, c_send.at[slot], c_recv.at[slot], c_peer)
    for d in [depth] + deeper:
        for s in (side, 1 - side):
            arrived(dp_index(d, s, 1 - core), c_recv.at[2 * d + s])
    keep.wait()
    for copy in sends:
        copy.wait_send()


def gather_dp(own):
    size = lax.axis_size("dp")
    layers = size // 4
    sem = pltpu.SemaphoreType.DMA
    full = pl.pallas_call(
        lambda *refs: gather_kernel(layers, *refs),
        out_shape=jax.ShapeDtypeStruct((size,) + own.shape, own.dtype),
        in_specs=[pl.BlockSpec(memory_space=pltpu.VMEM)],
        out_specs=pl.BlockSpec(memory_space=pltpu.VMEM),
        scratch_shapes=[
            sem((layers,)), sem((layers,)), sem((layers,)), sem((layers,)),
            sem((2 * layers,)), sem((2 * layers,)), sem,
        ],
        compiler_params=pltpu.CompilerParams(
            collective_id=1, has_side_effects=True, vmem_limit_bytes=40 * 1024 * 1024
        ),
        name="gather_dp",
    )(own)
    return full.reshape(size * own.shape[0], own.shape[1])


def reduce_kernel(
    layers, part_ref, out_ref, c_buf, y_out, y_buf, z_out, z_buf,
    c_send, c_recv, y_send, y_recv, z_send, z_recv,
):
    f32 = jnp.float32
    me, depth, side, core = dp_place(layers * 4)
    deeper = [lax.rem(depth + step, layers) for step in range(1, layers)]
    y_peer = dp_index(depth, 1 - side, core)
    c_peer = dp_index(depth, side, 1 - core)
    greet([("dp", dp_index(d, side, core)) for d in deeper] + [("dp", y_peer), ("dp", c_peer)])
    order = deeper + [depth]
    sends = []

    def start(src, dst, send, recv, target):
        copy = remote(src, dst, send, recv, target)
        copy.start()
        sends.append(copy)

    for s in (1 - side, side):
        for d in order:
            slot = 2 * d + s
            start(
                part_ref.at[dp_index(d, s, 1 - core)], c_buf.at[slot],
                c_send.at[slot], c_recv.at[slot], c_peer,
            )
    for d in order:
        slot = 2 * d + 1 - side
        remote(c_buf.at[slot], c_buf.at[slot], c_send.at[slot], c_recv.at[slot], c_peer).wait_recv()
        mine = part_ref[dp_index(d, 1 - side, core)].astype(f32)
        y_out[d] = (mine + c_buf[slot].astype(f32)).astype(y_out.dtype)
        start(y_out.at[d], y_buf.at[d], y_send.at[d], y_recv.at[d], y_peer)
    for d in order:
        slot = 2 * d + side
        remote(c_buf.at[slot], c_buf.at[slot], c_send.at[slot], c_recv.at[slot], c_peer).wait_recv()
        remote(y_buf.at[d], y_buf.at[d], y_send.at[d], y_recv.at[d], y_peer).wait_recv()
        total = part_ref[dp_index(d, side, core)].astype(f32) + c_buf[slot].astype(f32)
        total = total + y_buf[d].astype(f32)
        if d is not depth:
            z_out[d] = total.astype(z_out.dtype)
            start(
                z_out.at[d], z_buf.at[depth], z_send.at[d], z_recv.at[depth],
                dp_index(d, side, core),
            )
        else:
            out_ref[...] = total
    for d in deeper:
        remote(z_buf.at[d], z_buf.at[d], z_send.at[d], z_recv.at[d], y_peer).wait_recv()
        out_ref[...] += z_buf[d].astype(f32)
    for copy in sends:
        copy.wait_send()


def reduce_dp(part):
    size, rows, columns = part.shape
    layers = size // 4
    sem = pltpu.SemaphoreType.DMA
    block = lambda count: pltpu.VMEM((count, rows, columns), part.dtype)
    return pl.pallas_call(
        lambda *refs: reduce_kernel(layers, *refs),
        out_shape=jax.ShapeDtypeStruct((rows, columns), jnp.float32),
        in_specs=[pl.BlockSpec(memory_space=pltpu.VMEM)],
        out_specs=pl.BlockSpec(memory_space=pltpu.VMEM),
        scratch_shapes=[
            block(2 * layers), block(layers), block(layers), block(layers), block(layers),
            sem((2 * layers,)), sem((2 * layers,)), sem((layers,)), sem((layers,)),
            sem((layers,)), sem((layers,)),
        ],
        compiler_params=pltpu.CompilerParams(
            collective_id=2, has_side_effects=True, vmem_limit_bytes=60 * 1024 * 1024
        ),
        name="reduce_dp",
    )(part)


def swap(piece):
    return lax.ppermute(piece, "tensor", [(0, 1), (1, 0)])


def spread(piece):
    return jnp.concatenate([piece, swap(piece)], axis=0)


def mm(left, right, dims):
    return lax.dot_general(left, right, (dims, ((), ())), preferred_element_type=jnp.float32)


NN = ((1,), (0,))
NT = ((1,), (1,))
TN = ((0,), (0,))


def collect(lefts, rights, dims, own_rows):
    def term(first, last):
        total = None
        for left, right in zip(lefts, rights):
            now = mm(left[first:last], right, dims)
            total = now if total is None else total + now
        return total

    away = swap(term(own_rows, None).astype(jnp.bfloat16))
    return term(0, own_rows) + away.astype(jnp.float32)


def body(
    tokens,
    segment_ids,
    query_weight,
    key_weight,
    value_weight,
    out_weight,
    gate_weight,
    up_weight,
    down_weight,
    gain_before_attention,
    gain_after_attention,
    gain_before_feed,
    gain_after_feed,
    query_gain,
    key_gain,
    cotangent,
):
    f32 = jnp.float32
    bf16 = jnp.bfloat16
    own_rows = tokens.shape[0]
    total_rows = 2 * own_rows
    tensor_index = lax.axis_index("tensor")
    own_start = tensor_index * own_rows
    away_start = own_rows - own_start
    scale = HD ** (-0.5)
    shard_rows = key_weight.shape[0]
    head_rows = query_gain.shape[0]
    pad_head = lambda g: jnp.pad(g, (0, shard_rows - head_rows))
    gains = jnp.stack(
        [
            gain_before_attention, gain_after_attention, gain_before_feed, gain_after_feed,
            pad_head(query_gain), pad_head(key_gain),
        ],
        axis=1,
    )
    gains = jnp.pad(gains, ((0, 0), (0, 128 - gains.shape[1])))
    pieces = [query_weight, key_weight, value_weight, out_weight.T, gate_weight, up_weight, down_weight.T, gains]
    widths = [p.shape[1] for p in pieces]
    starts = [sum(widths[:i]) for i in range(len(widths) + 1)]
    full = gather_dp(jnp.concatenate(pieces, axis=1))
    query_full, key_full, value_full, out_t, gate_full, up_full, down_t, gain_full = [
        full[:, a:b] for a, b in zip(starts[:-1], starts[1:])
    ]
    gain_cols = gain_full[:, :8].astype(f32).T
    gain_ai, gain_ao, gain_fi, gain_fo = gain_cols[0], gain_cols[1], gain_cols[2], gain_cols[3]
    gain_query = gain_cols[4].reshape(-1, shard_rows)[:, :head_rows].reshape(-1)
    gain_key = gain_cols[5].reshape(-1, shard_rows)[:, :head_rows].reshape(-1)
    local_heads = query_full.shape[1] // HD
    offsets = jnp.arange(own_rows, dtype=jnp.int32)
    position = jnp.concatenate([own_start + offsets, away_start + offsets])
    segments = jnp.concatenate(
        [
            lax.dynamic_slice_in_dim(segment_ids, own_start, own_rows, 0),
            lax.dynamic_slice_in_dim(segment_ids, away_start, own_rows, 0),
        ]
    )
    x_rows = tokens.astype(f32)
    normed_in = spread(norm_fwd(x_rows, gain_ai).astype(bf16))
    queries = mm(normed_in, query_full, NN).reshape(total_rows, local_heads, HD)
    key_rows = mm(normed_in, key_full, NN)
    value_rows = mm(normed_in, value_full, NN).astype(bf16)
    cosine, sine_table = rope_tables(segments, position)
    query_rot = (
        rotate(norm_fwd(queries, gain_query), cosine[:, None, :], sine_table[:, None, :]) * scale
    ).astype(bf16)
    key_rot = rotate(norm_fwd(key_rows, gain_key), cosine, sine_table).astype(bf16)
    spacing = position[:, None] - position[None, :]
    allowed = (segments[:, None] == segments[None, :]) & (spacing >= 0) & (spacing < WINDOW)
    allowed = allowed[None]
    scores = jnp.einsum("qhd,kd->hqk", query_rot, key_rot, preferred_element_type=f32)
    exp_total = jnp.sum(jnp.where(allowed, jnp.exp(scores), 0.0), axis=-1, keepdims=True)
    log_total = jnp.log(exp_total)
    probs = jnp.where(allowed, jnp.exp(scores - log_total), 0.0)
    probs_b = probs.astype(bf16)
    attended = jnp.einsum("hqk,kd->qhd", probs_b, value_rows, preferred_element_type=f32)
    attended = attended.reshape(total_rows, local_heads * HD).astype(bf16)
    mixed = collect((attended,), (out_t,), NT, own_rows)
    hidden_state = x_rows + norm_fwd(mixed, gain_ao)
    normed_mid = spread(norm_fwd(hidden_state, gain_fi).astype(bf16))
    gate_pre = mm(normed_mid, gate_full, NN)
    up_values = mm(normed_mid, up_full, NN)
    gelu_value, gelu_slope = gelu_parts(gate_pre)
    activated = (gelu_value * up_values).astype(bf16)
    feed_out = collect((activated,), (down_t,), NT, own_rows)
    result = hidden_state + norm_fwd(feed_out, gain_fo)
    grad_feed, grad_gfo = norm_back(feed_out, gain_fo, cotangent)
    grad_feed_all = spread(grad_feed.astype(bf16))
    grad_act = mm(grad_feed_all, down_t, NN)
    grad_down_t = mm(grad_feed_all, activated, TN)
    grad_gate_b = (grad_act * up_values * gelu_slope).astype(bf16)
    grad_up_b = (grad_act * gelu_value).astype(bf16)
    grad_gate_w = mm(normed_mid, grad_gate_b, TN)
    grad_up_w = mm(normed_mid, grad_up_b, TN)
    grad_mid = collect((grad_gate_b, grad_up_b), (gate_full, up_full), NT, own_rows)
    grad_mid_in, grad_gfi = norm_back(hidden_state, gain_fi, grad_mid)
    grad_hidden = cotangent + grad_mid_in
    grad_mixed, grad_gao = norm_back(mixed, gain_ao, grad_hidden)
    grad_mixed_all = spread(grad_mixed.astype(bf16))
    grad_attended = mm(grad_mixed_all, out_t, NN).astype(bf16)
    grad_out_t = mm(grad_mixed_all, attended, TN)
    grad_heads = grad_attended.reshape(total_rows, local_heads, HD)
    grad_probs = jnp.einsum("qhd,kd->hqk", grad_heads, value_rows, preferred_element_type=f32)
    grad_scores = (
        probs * (grad_probs - jnp.sum(probs * grad_probs, axis=-1, keepdims=True))
    ).astype(bf16)
    grad_qrot = jnp.einsum("hqk,kd->qhd", grad_scores, key_rot, preferred_element_type=f32)
    grad_krot = jnp.einsum("hqk,qhd->kd", grad_scores, query_rot, preferred_element_type=f32)
    grad_vpart = jnp.einsum("hqk,qhd->kd", probs_b, grad_heads, preferred_element_type=f32)
    pair = jnp.concatenate([grad_krot, grad_vpart], axis=1)
    pair_away = swap(pair[own_rows:].astype(bf16)).astype(f32)
    pair_own = pair[:own_rows] + pair_away
    grad_kunit = unrotate(pair_own[:, :HD], cosine[:own_rows], sine_table[:own_rows])
    grad_value_b = pair_own[:, HD:].astype(bf16)
    grad_qunit = unrotate(grad_qrot * scale, cosine[:, None, :], sine_table[:, None, :])
    grad_queries, grad_gq = norm_back(queries, gain_query, grad_qunit)
    grad_keys, grad_gk = norm_back(key_rows[:own_rows], gain_key, grad_kunit)
    grad_queries_b = grad_queries.reshape(total_rows, local_heads * HD).astype(bf16)
    grad_keys_b = grad_keys.astype(bf16)
    normed_own = normed_in[:own_rows]
    grad_query_w = mm(normed_in, grad_queries_b, TN)
    grad_key_w = mm(normed_own, grad_keys_b, TN)
    grad_value_w = mm(normed_own, grad_value_b, TN)
    grad_normed = (
        collect((grad_queries_b,), (query_full,), NT, own_rows)
        + mm(grad_keys_b, key_full, NT)
        + mm(grad_value_b, value_full, NT)
    )
    grad_in_rows, grad_gai = norm_back(x_rows, gain_ai, grad_normed)
    grad_tokens = grad_hidden + grad_in_rows
    pad_gain = lambda g: jnp.pad(
        g.reshape(-1, head_rows), ((0, 0), (0, shard_rows - head_rows))
    ).reshape(-1)
    gain_grads = jnp.stack(
        [grad_gai, grad_gao, grad_gfi, grad_gfo, pad_gain(grad_gq), pad_gain(grad_gk)], axis=1
    )
    gain_grads = jnp.pad(gain_grads, ((0, 0), (0, 128 - gain_grads.shape[1])))
    parts = [
        grad_query_w, grad_key_w, grad_value_w, grad_out_t, grad_gate_w, grad_up_w, grad_down_t,
        gain_grads,
    ]
    packed = jnp.concatenate([p.astype(bf16) for p in parts], axis=1)
    total = reduce_dp(packed.reshape(-1, shard_rows, packed.shape[1]))
    shards = [total[:, a:b] for a, b in zip(starts[:-1], starts[1:])]
    shared = jnp.concatenate([shards[1], shards[2], shards[7]], axis=1)
    shared = shared + swap(shared)
    key_shard = shared[:, :HD]
    value_shard = shared[:, HD : 2 * HD]
    gain_shard = shared[:, 2 * HD :]
    return (
        result,
        grad_tokens,
        shards[0],
        key_shard,
        value_shard,
        shards[3].T,
        shards[4],
        shards[5],
        shards[6].T,
        gain_shard[:, 0],
        gain_shard[:, 1],
        gain_shard[:, 2],
        gain_shard[:, 3],
        gain_shard[:head_rows, 4],
        gain_shard[:head_rows, 5],
    )


def solution(mesh):
    in_specs = (
        P(("dp", "tensor"), None),
        P("dp"),
        P("dp", "tensor"),
        P("dp", None),
        P("dp", None),
        P("tensor", "dp"),
        P("dp", "tensor"),
        P("dp", "tensor"),
        P("tensor", "dp"),
        P("dp"),
        P("dp"),
        P("dp"),
        P("dp"),
        P("dp"),
        P("dp"),
        P(("dp", "tensor"), None),
    )
    out_specs = (
        P(("dp", "tensor"), None),
        P(("dp", "tensor"), None),
        P("dp", "tensor"),
        P("dp", None),
        P("dp", None),
        P("tensor", "dp"),
        P("dp", "tensor"),
        P("dp", "tensor"),
        P("tensor", "dp"),
        P("dp"),
        P("dp"),
        P("dp"),
        P("dp"),
        P("dp"),
        P("dp"),
    )
    return jax.shard_map(body, mesh=mesh, in_specs=in_specs, out_specs=out_specs, check_vma=False)
```

```python
import math

import jax
import jax.numpy as jnp
from jax import lax
from jax.experimental import pallas as pl
from jax.experimental.pallas import tpu as pltpu
from jax.sharding import PartitionSpec as P

HD = 256
WINDOW = 512


EPS = 1e-06
ROPE_BASE = 10000.0


def norm_fwd(values, gain):
    inverse = lax.rsqrt(jnp.mean(values * values, axis=-1, keepdims=True) + EPS)
    return values * inverse * gain


def norm_back(values, gain, grad_out):
    inverse = lax.rsqrt(jnp.mean(values * values, axis=-1, keepdims=True) + EPS)
    unit_rows = values * inverse
    scaled = grad_out * gain
    grad_in = inverse * (scaled - unit_rows * jnp.mean(scaled * unit_rows, axis=-1, keepdims=True))
    grad_gain = jnp.sum((grad_out * unit_rows).reshape(-1, values.shape[-1]), axis=0)
    return (grad_in, grad_gain)


def gelu_parts(gate_pre):
    factor = math.sqrt(2.0 / math.pi)
    tangent = jnp.tanh(factor * (gate_pre + 0.044715 * gate_pre * gate_pre * gate_pre))
    value_out = 0.5 * gate_pre * (1.0 + tangent)
    slope = 0.5 * (1.0 + tangent) + 0.5 * gate_pre * (1.0 - tangent * tangent) * factor * (
        1.0 + 3.0 * 0.044715 * gate_pre * gate_pre
    )
    return (value_out, slope)


def rope_tables(segments, position):
    earlier = jnp.sum((segments[None, :] < segments[:, None]).astype(jnp.int32), axis=1)
    place = (position - earlier).astype(jnp.float32)
    half_width = HD // 2
    freq = jnp.exp(-(2.0 * jnp.arange(half_width, dtype=jnp.float32) / HD) * math.log(ROPE_BASE))
    angle = place[:, None] * freq[None, :]
    return (jnp.cos(angle), jnp.sin(angle))


def rotate(vals, cosine, sine_table):
    half_width = vals.shape[-1] // 2
    first_half = vals[..., :half_width]
    second = vals[..., half_width:]
    return jnp.concatenate(
        [first_half * cosine - second * sine_table, second * cosine + first_half * sine_table],
        axis=-1,
    )


def unrotate(grads, cosine, sine_table):
    half_width = grads.shape[-1] // 2
    first_half = grads[..., :half_width]
    second = grads[..., half_width:]
    return jnp.concatenate(
        [first_half * cosine + second * sine_table, second * cosine - first_half * sine_table],
        axis=-1,
    )


def greet(partners):
    barrier = pltpu.get_barrier_semaphore()
    for axis, index in partners:
        pl.semaphore_signal(
            barrier, inc=1, device_id={axis: index}, device_id_type=pl.DeviceIdType.MESH
        )
    pl.semaphore_wait(barrier, len(partners))


def dp_place(size):
    me = lax.axis_index("dp")
    core = lax.rem(me, 2)
    side = lax.rem(me // 2, 2)
    depth = me // 4
    return me, depth, side, core


def dp_index(depth, side, core):
    return depth * 4 + side * 2 + core


def remote(src, dst, send, recv, index):
    return pltpu.make_async_remote_copy(
        src_ref=src,
        dst_ref=dst,
        send_sem=send,
        recv_sem=recv,
        device_id={"dp": index},
        device_id_type=pl.DeviceIdType.MESH,
    )


def gather_kernel(layers, own_ref, full_ref, z_send, z_recv, y_send, y_recv, c_send, c_recv, local):
    me, depth, side, core = dp_place(layers * 4)
    deeper = [lax.rem(depth + step, layers) for step in range(1, layers)]
    y_peer = dp_index(depth, 1 - side, core)
    c_peer = dp_index(depth, side, 1 - core)
    greet([("dp", dp_index(d, side, core)) for d in deeper] + [("dp", y_peer), ("dp", c_peer)])
    sends = []

    def start(src, index, send, recv, target):
        copy = remote(src, full_ref.at[index], send, recv, target)
        copy.start()
        sends.append(copy)

    def arrived(index, recv):
        remote(full_ref.at[index], full_ref.at[index], local, recv, y_peer).wait_recv()

    keep = pltpu.make_async_copy(own_ref, full_ref.at[me], local)
    keep.start()
    start(own_ref, me, y_send.at[depth], y_recv.at[depth], y_peer)
    for d in deeper:
        start(own_ref, me, z_send.at[d], z_recv.at[depth], dp_index(d, side, core))
    start(own_ref, me, c_send.at[2 * depth + side], c_recv.at[2 * depth + side], c_peer)
    for d in deeper:
        index = dp_index(d, side, core)
        arrived(index, z_recv.at[d])
        start(full_ref.at[index], index, y_send.at[d], y_recv.at[d], y_peer)
        slot = 2 * d + side
        start(full_ref.at[index], index, c_send.at[slot], c_recv.at[slot], c_peer)
    for d in [depth] + deeper:
        index = dp_index(d, 1 - side, core)
        arrived(index, y_recv.at[d])
        slot = 2 * d + 1 - side
        start(full_ref.at[index], index, c_send.at[slot], c_recv.at[slot], c_peer)
    for d in [depth] + deeper:
        for s in (side, 1 - side):
            arrived(dp_index(d, s, 1 - core), c_recv.at[2 * d + s])
    keep.wait()
    for copy in sends:
        copy.wait_send()


def gather_dp(own):
    size = lax.axis_size("dp")
    layers = size // 4
    sem = pltpu.SemaphoreType.DMA
    full = pl.pallas_call(
        lambda *refs: gather_kernel(layers, *refs),
        out_shape=jax.ShapeDtypeStruct((size,) + own.shape, own.dtype),
        in_specs=[pl.BlockSpec(memory_space=pltpu.VMEM)],
        out_specs=pl.BlockSpec(memory_space=pltpu.VMEM),
        scratch_shapes=[
            sem((layers,)), sem((layers,)), sem((layers,)), sem((layers,)),
            sem((2 * layers,)), sem((2 * layers,)), sem,
        ],
        compiler_params=pltpu.CompilerParams(
            collective_id=1, has_side_effects=True, vmem_limit_bytes=40 * 1024 * 1024
        ),
        name="gather_dp",
    )(own)
    return full.reshape(size * own.shape[0], own.shape[1])


def reduce_kernel(
    layers, part_ref, out_ref, c_buf, y_out, y_buf, z_out, z_buf,
    c_send, c_recv, y_send, y_recv, z_send, z_recv,
):
    f32 = jnp.float32
    me, depth, side, core = dp_place(layers * 4)
    deeper = [lax.rem(depth + step, layers) for step in range(1, layers)]
    y_peer = dp_index(depth, 1 - side, core)
    c_peer = dp_index(depth, side, 1 - core)
    greet([("dp", dp_index(d, side, core)) for d in deeper] + [("dp", y_peer), ("dp", c_peer)])
    order = deeper + [depth]
    sends = []

    def start(src, dst, send, recv, target):
        copy = remote(src, dst, send, recv, target)
        copy.start()
        sends.append(copy)

    for s in (1 - side, side):
        for d in order:
            slot = 2 * d + s
            start(
                part_ref.at[dp_index(d, s, 1 - core)], c_buf.at[slot],
                c_send.at[slot], c_recv.at[slot], c_peer,
            )
    for d in order:
        slot = 2 * d + 1 - side
        remote(c_buf.at[slot], c_buf.at[slot], c_send.at[slot], c_recv.at[slot], c_peer).wait_recv()
        mine = part_ref[dp_index(d, 1 - side, core)].astype(f32)
        y_out[d] = (mine + c_buf[slot].astype(f32)).astype(y_out.dtype)
        start(y_out.at[d], y_buf.at[d], y_send.at[d], y_recv.at[d], y_peer)
    for d in order:
        slot = 2 * d + side
        remote(c_buf.at[slot], c_buf.at[slot], c_send.at[slot], c_recv.at[slot], c_peer).wait_recv()
        remote(y_buf.at[d], y_buf.at[d], y_send.at[d], y_recv.at[d], y_peer).wait_recv()
        total = part_ref[dp_index(d, side, core)].astype(f32) + c_buf[slot].astype(f32)
        total = total + y_buf[d].astype(f32)
        if d is not depth:
            z_out[d] = total.astype(z_out.dtype)
            start(
                z_out.at[d], z_buf.at[depth], z_send.at[d], z_recv.at[depth],
                dp_index(d, side, core),
            )
        else:
            out_ref[...] = total
    for d in deeper:
        remote(z_buf.at[d], z_buf.at[d], z_send.at[d], z_recv.at[d], y_peer).wait_recv()
        out_ref[...] += z_buf[d].astype(f32)
    for copy in sends:
        copy.wait_send()


def reduce_dp(part):
    size, rows, columns = part.shape
    layers = size // 4
    sem = pltpu.SemaphoreType.DMA
    block = lambda count: pltpu.VMEM((count, rows, columns), part.dtype)
    return pl.pallas_call(
        lambda *refs: reduce_kernel(layers, *refs),
        out_shape=jax.ShapeDtypeStruct((rows, columns), jnp.float32),
        in_specs=[pl.BlockSpec(memory_space=pltpu.VMEM)],
        out_specs=pl.BlockSpec(memory_space=pltpu.VMEM),
        scratch_shapes=[
            block(2 * layers), block(layers), block(layers), block(layers), block(layers),
            sem((2 * layers,)), sem((2 * layers,)), sem((layers,)), sem((layers,)),
            sem((layers,)), sem((layers,)),
        ],
        compiler_params=pltpu.CompilerParams(
            collective_id=2, has_side_effects=True, vmem_limit_bytes=60 * 1024 * 1024
        ),
        name="reduce_dp",
    )(part)


def pair_up(arr, bit):
    size = lax.axis_size("dp")
    return lax.ppermute(arr, "dp", [(i, i ^ (1 << bit)) for i in range(size)])


def gather_bits(piece, order):
    bits = len(order)
    me = lax.axis_index("dp")
    arr = piece.reshape((1,) * bits + piece.shape)
    for bit in order:
        other = pair_up(arr, bit)
        low = lax.rem(me // (1 << bit), 2) == 0
        arr = jnp.concatenate(
            [jnp.where(low, arr, other), jnp.where(low, other, arr)], axis=bits - 1 - bit
        )
    return arr.reshape(-1, piece.shape[-1])


def reduce_steps(part, order):
    bits = len(order)
    me = lax.axis_index("dp")
    size = lax.axis_size("dp")
    arr = part.reshape((2,) * bits + (part.shape[0] // size, part.shape[1]))

    def step(arr, bit, last):
        mine = lax.rem(me // (1 << bit), 2)
        axis = bits - 1 - bit
        other = pair_up(lax.dynamic_slice_in_dim(arr, 1 - mine, 1, axis), bit)
        kept = lax.dynamic_slice_in_dim(arr, mine, 1, axis)
        arr = kept.astype(jnp.float32) + other.astype(jnp.float32)
        return arr if last else arr.astype(part.dtype)

    return arr, [lambda arr, bit=bit: step(arr, bit, bit == order[-1]) for bit in order]


def tie(value, *streams):
    return lax.optimization_barrier((value,) + streams)


def bit_orders():
    bits = lax.axis_size("dp").bit_length() - 1
    deep = list(range(2, bits))
    return ([1] + deep[::-1] + [0], deep[::-1] + [1, 0], [0, 1] + deep, [0] + deep + [1])


def swap(piece):
    return lax.ppermute(piece, "tensor", [(0, 1), (1, 0)])


def spread(piece):
    return jnp.concatenate([piece, swap(piece)], axis=0)


def mm(left, right, dims):
    return lax.dot_general(left, right, (dims, ((), ())), preferred_element_type=jnp.float32)


NN = ((1,), (0,))
NT = ((1,), (1,))
TN = ((0,), (0,))


def collect(lefts, rights, dims, own_rows):
    def term(first, last):
        total = None
        for left, right in zip(lefts, rights):
            now = mm(left[first:last], right, dims)
            total = now if total is None else total + now
        return total

    away = swap(term(own_rows, None).astype(jnp.bfloat16))
    return term(0, own_rows) + away.astype(jnp.float32)


def body(
    tokens,
    segment_ids,
    query_weight,
    key_weight,
    value_weight,
    out_weight,
    gate_weight,
    up_weight,
    down_weight,
    gain_before_attention,
    gain_after_attention,
    gain_before_feed,
    gain_after_feed,
    query_gain,
    key_gain,
    cotangent,
):
    f32 = jnp.float32
    bf16 = jnp.bfloat16
    own_rows = tokens.shape[0]
    total_rows = 2 * own_rows
    tensor_index = lax.axis_index("tensor")
    own_start = tensor_index * own_rows
    away_start = own_rows - own_start
    scale = HD ** (-0.5)
    shard_rows = key_weight.shape[0]
    head_rows = query_gain.shape[0]
    pad_head = lambda g: jnp.pad(g, (0, shard_rows - head_rows))
    gains = jnp.stack(
        [
            gain_before_attention, gain_after_attention, gain_before_feed, gain_after_feed,
            pad_head(query_gain), pad_head(key_gain),
        ],
        axis=1,
    )
    gains = jnp.pad(gains, ((0, 0), (0, 128 - gains.shape[1])))
    side_first, deep_first, side_reduce, deep_reduce = bit_orders()
    pieces = [query_weight, key_weight, value_weight, out_weight.T, gains]
    widths = [p.shape[1] for p in pieces]
    starts = [sum(widths[:i]) for i in range(len(widths) + 1)]
    full = gather_dp(jnp.concatenate(pieces, axis=1))
    query_full, key_full, value_full, out_t, gain_full = [
        full[:, a:b] for a, b in zip(starts[:-1], starts[1:])
    ]
    hidden = gate_weight.shape[1]
    gate_up = gather_bits(jnp.concatenate([gate_weight, up_weight], axis=1), side_first)
    gate_full, up_full = gate_up[:, :hidden], gate_up[:, hidden:]
    down_t = gather_bits(down_weight.T, deep_first)
    gain_cols = gain_full[:, :8].astype(f32).T
    gain_ai, gain_ao, gain_fi, gain_fo = gain_cols[0], gain_cols[1], gain_cols[2], gain_cols[3]
    gain_query = gain_cols[4].reshape(-1, shard_rows)[:, :head_rows].reshape(-1)
    gain_key = gain_cols[5].reshape(-1, shard_rows)[:, :head_rows].reshape(-1)
    local_heads = query_full.shape[1] // HD
    offsets = jnp.arange(own_rows, dtype=jnp.int32)
    position = jnp.concatenate([own_start + offsets, away_start + offsets])
    segments = jnp.concatenate(
        [
            lax.dynamic_slice_in_dim(segment_ids, own_start, own_rows, 0),
            lax.dynamic_slice_in_dim(segment_ids, away_start, own_rows, 0),
        ]
    )
    x_rows = tokens.astype(f32)
    normed_in = spread(norm_fwd(x_rows, gain_ai).astype(bf16))
    queries = mm(normed_in, query_full, NN).reshape(total_rows, local_heads, HD)
    key_rows = mm(normed_in, key_full, NN)
    value_rows = mm(normed_in, value_full, NN).astype(bf16)
    cosine, sine_table = rope_tables(segments, position)
    query_rot = (
        rotate(norm_fwd(queries, gain_query), cosine[:, None, :], sine_table[:, None, :]) * scale
    ).astype(bf16)
    key_rot = rotate(norm_fwd(key_rows, gain_key), cosine, sine_table).astype(bf16)
    spacing = position[:, None] - position[None, :]
    allowed = (segments[:, None] == segments[None, :]) & (spacing >= 0) & (spacing < WINDOW)
    allowed = allowed[None]
    scores = jnp.einsum("qhd,kd->hqk", query_rot, key_rot, preferred_element_type=f32)
    exp_total = jnp.sum(jnp.where(allowed, jnp.exp(scores), 0.0), axis=-1, keepdims=True)
    log_total = jnp.log(exp_total)
    probs = jnp.where(allowed, jnp.exp(scores - log_total), 0.0)
    probs_b = probs.astype(bf16)
    attended = jnp.einsum("hqk,kd->qhd", probs_b, value_rows, preferred_element_type=f32)
    attended = attended.reshape(total_rows, local_heads * HD).astype(bf16)
    mixed = collect((attended,), (out_t,), NT, own_rows)
    hidden_state = x_rows + norm_fwd(mixed, gain_ao)
    normed_mid = spread(norm_fwd(hidden_state, gain_fi).astype(bf16))
    gate_pre = mm(normed_mid, gate_full, NN)
    up_values = mm(normed_mid, up_full, NN)
    gelu_value, gelu_slope = gelu_parts(gate_pre)
    activated = (gelu_value * up_values).astype(bf16)
    feed_out = collect((activated,), (down_t,), NT, own_rows)
    result = hidden_state + norm_fwd(feed_out, gain_fo)
    grad_feed, grad_gfo = norm_back(feed_out, gain_fo, cotangent)
    grad_feed_all = spread(grad_feed.astype(bf16))
    grad_act = mm(grad_feed_all, down_t, NN)
    grad_down_t = mm(grad_feed_all, activated, TN)
    grad_gate_b = (grad_act * up_values * gelu_slope).astype(bf16)
    grad_up_b = (grad_act * gelu_value).astype(bf16)
    grad_gate_w = mm(normed_mid, grad_gate_b, TN)
    grad_up_w = mm(normed_mid, grad_up_b, TN)
    down_red, down_steps = reduce_steps(grad_down_t.astype(bf16), deep_reduce)
    gate_up_red, gate_up_steps = reduce_steps(
        jnp.concatenate([grad_gate_w.astype(bf16), grad_up_w.astype(bf16)], axis=1), side_reduce
    )
    grad_mid = collect((grad_gate_b, grad_up_b), (gate_full, up_full), NT, own_rows)
    down_red = down_steps[0](down_red)
    gate_up_red = gate_up_steps[0](gate_up_red)
    grad_mid, down_red, gate_up_red = tie(grad_mid, down_red, gate_up_red)
    down_red = down_steps[1](down_red)
    gate_up_red = gate_up_steps[1](gate_up_red)
    grad_mid_in, grad_gfi = norm_back(hidden_state, gain_fi, grad_mid)
    grad_hidden = cotangent + grad_mid_in
    grad_mixed, grad_gao = norm_back(mixed, gain_ao, grad_hidden)
    grad_mixed_all = spread(grad_mixed.astype(bf16))
    grad_mixed_all, down_red = tie(grad_mixed_all, down_red)
    down_red = down_steps[2](down_red)
    grad_attended = mm(grad_mixed_all, out_t, NN).astype(bf16)
    grad_out_t = mm(grad_mixed_all, attended, TN)
    grad_heads = grad_attended.reshape(total_rows, local_heads, HD)
    grad_probs = jnp.einsum("qhd,kd->hqk", grad_heads, value_rows, preferred_element_type=f32)
    grad_scores = (
        probs * (grad_probs - jnp.sum(probs * grad_probs, axis=-1, keepdims=True))
    ).astype(bf16)
    grad_scores, down_red, gate_up_red = tie(grad_scores, down_red, gate_up_red)
    for step in down_steps[3:]:
        down_red = step(down_red)
    gate_up_red = gate_up_steps[2](gate_up_red)
    grad_qrot = jnp.einsum("hqk,kd->qhd", grad_scores, key_rot, preferred_element_type=f32)
    grad_krot = jnp.einsum("hqk,qhd->kd", grad_scores, query_rot, preferred_element_type=f32)
    grad_vpart = jnp.einsum("hqk,qhd->kd", probs_b, grad_heads, preferred_element_type=f32)
    pair = jnp.concatenate([grad_krot, grad_vpart], axis=1)
    pair_away = swap(pair[own_rows:].astype(bf16)).astype(f32)
    pair_own = pair[:own_rows] + pair_away
    pair_own, down_red, gate_up_red = tie(pair_own, down_red, gate_up_red)
    for step in gate_up_steps[3:]:
        gate_up_red = step(gate_up_red)
    down_shard = down_red.reshape(down_red.shape[-2:])
    gate_up_shard = gate_up_red.reshape(gate_up_red.shape[-2:])
    grad_kunit = unrotate(pair_own[:, :HD], cosine[:own_rows], sine_table[:own_rows])
    grad_value_b = pair_own[:, HD:].astype(bf16)
    grad_qunit = unrotate(grad_qrot * scale, cosine[:, None, :], sine_table[:, None, :])
    grad_queries, grad_gq = norm_back(queries, gain_query, grad_qunit)
    grad_keys, grad_gk = norm_back(key_rows[:own_rows], gain_key, grad_kunit)
    grad_queries_b = grad_queries.reshape(total_rows, local_heads * HD).astype(bf16)
    grad_keys_b = grad_keys.astype(bf16)
    normed_own = normed_in[:own_rows]
    grad_query_w = mm(normed_in, grad_queries_b, TN)
    grad_key_w = mm(normed_own, grad_keys_b, TN)
    grad_value_w = mm(normed_own, grad_value_b, TN)
    grad_normed = (
        collect((grad_queries_b,), (query_full,), NT, own_rows)
        + mm(grad_keys_b, key_full, NT)
        + mm(grad_value_b, value_full, NT)
    )
    grad_in_rows, grad_gai = norm_back(x_rows, gain_ai, grad_normed)
    grad_tokens = grad_hidden + grad_in_rows
    pad_gain = lambda g: jnp.pad(
        g.reshape(-1, head_rows), ((0, 0), (0, shard_rows - head_rows))
    ).reshape(-1)
    gain_grads = jnp.stack(
        [grad_gai, grad_gao, grad_gfi, grad_gfo, pad_gain(grad_gq), pad_gain(grad_gk)], axis=1
    )
    gain_grads = jnp.pad(gain_grads, ((0, 0), (0, 128 - gain_grads.shape[1])))
    parts = [
        grad_query_w, grad_key_w, grad_value_w, grad_out_t, gain_grads,
    ]
    packed = jnp.concatenate([p.astype(bf16) for p in parts], axis=1)
    total = reduce_dp(packed.reshape(-1, shard_rows, packed.shape[1]))
    shards = [total[:, a:b] for a, b in zip(starts[:-1], starts[1:])]
    shared = jnp.concatenate([shards[1], shards[2], shards[4]], axis=1)
    shared = shared + swap(shared)
    key_shard = shared[:, :HD]
    value_shard = shared[:, HD : 2 * HD]
    gain_shard = shared[:, 2 * HD :]
    return (
        result,
        grad_tokens,
        shards[0],
        key_shard,
        value_shard,
        shards[3].T,
        gate_up_shard[:, :hidden],
        gate_up_shard[:, hidden:],
        down_shard.T,
        gain_shard[:, 0],
        gain_shard[:, 1],
        gain_shard[:, 2],
        gain_shard[:, 3],
        gain_shard[:head_rows, 4],
        gain_shard[:head_rows, 5],
    )


def solution(mesh):
    in_specs = (
        P(("dp", "tensor"), None),
        P("dp"),
        P("dp", "tensor"),
        P("dp", None),
        P("dp", None),
        P("tensor", "dp"),
        P("dp", "tensor"),
        P("dp", "tensor"),
        P("tensor", "dp"),
        P("dp"),
        P("dp"),
        P("dp"),
        P("dp"),
        P("dp"),
        P("dp"),
        P(("dp", "tensor"), None),
    )
    out_specs = (
        P(("dp", "tensor"), None),
        P(("dp", "tensor"), None),
        P("dp", "tensor"),
        P("dp", None),
        P("dp", None),
        P("tensor", "dp"),
        P("dp", "tensor"),
        P("dp", "tensor"),
        P("tensor", "dp"),
        P("dp"),
        P("dp"),
        P("dp"),
        P("dp"),
        P("dp"),
        P("dp"),
    )
    return jax.shard_map(body, mesh=mesh, in_specs=in_specs, out_specs=out_specs, check_vma=False)
```
